512 devices in a mesh: dp: 8 (over y, core), expert: 64 (over x, z).
Axes of the slice: x: 4, y: 4, z: 16, core: 2. Of those that a mesh axis runs over, the one named last changes fastest.
Arguments:
- layer_in: bfloat16 [2048, 4096], P('expert', 'dp'), may hold values from -6 to 6
- grad_out: bfloat16 [2048, 4096], P('expert', 'dp'), may hold values from -6 to 6
- gate_prob: float32 [2048, 8], P('expert'), may hold values from 0.05 to 0.6
- expert_ids: int32 [2048, 8], P('expert'), may hold values from 0 to 31, as said below
- replica_index: int32 [2048, 8], P('expert'), may hold values from 0 to 3, as said below
- slot_expert: int32 [64], replicated, may hold values from 0 to 31, as said below
- w_gate: bfloat16 [64, 4096, 1024], P('expert', None, 'dp')
- w_up: bfloat16 [64, 4096, 1024], P('expert', None, 'dp')
- w_down: bfloat16 [64, 1024, 4096], P('expert', 'dp')
Outputs:
- grad_in: bfloat16 [2048, 4096], P('expert', 'dp')
- grad_w_down: bfloat16 [64, 1024, 4096], P('expert', 'dp')
The draws below stay inside these ranges and needn't reach their ends.
Inputs may be any that keep to these rules, and one draw needn't show every extreme that they name: `slot_expert`: every expert owns one run of consecutive slots, counted cyclically (slot 63 is followed by slot 0), of 1 to 4 slots; the runs cover all 64 slots. `expert_ids`: the 8 experts of one token are different. `replica_index`: each entry is below the number of slots of the expert of the same choice. Of the 32 tokens of one index of expert, at most 8 choices go to any one slot, and in every draw some slot receives exactly 8 from the tokens of every index of expert.
All inputs are finite; a program needn't handle non-finite values.
Results may differ from the reference program's by a relative error of at most 0.014.
Values may be sent and summed in bfloat16 or wider, within the bound.
No kernel may reach another device: no remote copies, remote signals or barrier semaphores. Data moves between devices by JAX's collectives and lax.ppermute only.
A program may use at most 64 MiB of HBM per device.

```python
import math
import jax
import jax.numpy as jnp
from jax import lax

D = 4096
FF = 1024
TOP = 8
TOK_E = 32
SLOTS = 64
MAXREP = 4
EXPERTS = 32
CAP = 8
RECV = 512
TOKENS = 2048
N_DP = 8


def routing_tables(key):
    hot_rank = jax.random.permutation(jax.random.fold_in(key, 71), EXPERTS).astype(jnp.int32)
    replicas = jnp.where(hot_rank < SLOTS // 8, MAXREP, jnp.where(hot_rank < SLOTS // 4, 2, 1)).astype(jnp.int32)
    shuffle = jax.random.permutation(jax.random.fold_in(key, 72), EXPERTS).astype(jnp.int32)
    shuffle = jnp.where(hot_rank < 2, EXPERTS, shuffle)
    order_key = hot_rank % 2 * (2 * EXPERTS + 2) + shuffle
    run_order = jnp.argsort(order_key, stable=True).astype(jnp.int32)
    run_length = replicas[run_order]
    run_end = jnp.cumsum(run_length).astype(jnp.int32)
    run_start = (run_end - run_length).astype(jnp.int32)
    slot_index = jnp.arange(SLOTS, dtype=jnp.int32)
    slot_run = jnp.sum((run_end[None, :] <= slot_index[:, None]).astype(jnp.int32), axis=1)
    roll_by = min(2, MAXREP - 1)
    slot_expert = jnp.roll(run_order[slot_run], roll_by).astype(jnp.int32)
    first_slot = jnp.zeros((EXPERTS,), jnp.int32).at[run_order].set((run_start + roll_by) % SLOTS)
    hot_expert = jnp.argmax(hot_rank == 0).astype(jnp.int32)
    forced_low = first_slot[hot_expert]
    forced_high = (forced_low + MAXREP - 1) % SLOTS
    pairing = jax.random.permutation(jax.random.fold_in(key, 73), SLOTS).astype(jnp.int32)
    place_high = jnp.argmax(pairing == forced_high)
    pairing = pairing.at[place_high].set(pairing[0]).at[0].set(forced_high)
    place_low = jnp.argmax(pairing == forced_low)
    pairing = pairing.at[place_low].set(pairing[1]).at[1].set(forced_low)
    mean_load = TOP * TOK_E // SLOTS
    spread_top = max(CAP - mean_load - 1, 0)
    pair_heat = jax.random.randint(jax.random.fold_in(key, 74), (SLOTS // 2,), 0, spread_top + 1)
    jitter = jax.random.randint(jax.random.fold_in(key, 75), (SLOTS, SLOTS // 2), -1, 2)
    offset = jnp.clip(pair_heat[None, :] + jitter, 0, spread_top).astype(jnp.int32)
    offset = offset.at[:, 0].set(CAP - mean_load)
    loads = jnp.zeros((SLOTS, SLOTS), jnp.int32)
    loads = loads.at[:, pairing[0::2]].set(mean_load + offset)
    loads = loads.at[:, pairing[1::2]].set(mean_load - offset)
    block_base = jax.random.fold_in(key, 76)

    def fill_block(block_id, block_loads):
        block_key = jax.random.fold_in(block_base, block_id)
        token_perm = jax.random.permutation(jax.random.fold_in(block_key, 1), TOK_E).astype(jnp.int32)
        rotation = jax.random.randint(jax.random.fold_in(block_key, 2), (TOK_E,), 0, TOP)
        load_end = jnp.cumsum(block_loads).astype(jnp.int32)
        place = jnp.arange(TOP * TOK_E, dtype=jnp.int32)
        slot_of = jnp.sum((load_end[None, :] <= place[:, None]).astype(jnp.int32), axis=1)
        token_here = token_perm[place % TOK_E]
        column_here = (place // TOK_E + rotation[token_here]) % TOP
        expert_here = slot_expert[slot_of]
        replica_here = (slot_of - first_slot[expert_here]) % SLOTS
        chosen = jnp.zeros((TOK_E, TOP), jnp.int32).at[token_here, column_here].set(expert_here)
        replica_table = jnp.zeros((TOK_E, TOP), jnp.int32).at[token_here, column_here].set(replica_here)
        return (chosen, replica_table)
    chosen, replica_table = jax.vmap(fill_block)(slot_index, loads)
    return (slot_expert, chosen.reshape(TOKENS, TOP), replica_table.reshape(TOKENS, TOP))


def slot_weights(key, salt, height, breadth, fan_in):
    slot_expert = routing_tables(key)[0]
    base = jax.random.fold_in(key, salt)

    def one_matrix(expert):
        sub_key = jax.random.fold_in(base, expert)
        values = jax.random.normal(sub_key, (height, breadth), jnp.float32)
        return values * fan_in ** (-0.5)
    return jax.vmap(one_matrix)(slot_expert)


def draw_slot_expert(key, part):
    return routing_tables(key)[0]


def draw_expert_ids(key, part):
    return routing_tables(key)[1]


def draw_replica_index(key, part):
    return routing_tables(key)[2]


def draw_w_gate(key, part):
    return slot_weights(key, 501, D, FF, D).astype(jnp.bfloat16)


def draw_w_up(key, part):
    return slot_weights(key, 502, D, FF, D).astype(jnp.bfloat16)


def draw_w_down(key, part):
    return slot_weights(key, 503, FF, D, FF).astype(jnp.bfloat16)


def block_levels(key, shape, split, low, high):
    def one(position, blocks):
        draws = jax.random.uniform(jax.random.fold_in(jax.random.fold_in(key, 6), position), (blocks,), jnp.float32, low / len(split), high / len(split))
        return jnp.repeat(jnp.exp(draws), shape[position] // blocks).reshape((-1,) + (1,) * (len(shape) - position - 1))

    gain = one(*split[0])
    for cut in split[1:]:
        gain = gain * one(*cut)
    return gain


def noise(rng, extent, width, most, cuts=(), held_as=jnp.bfloat16):
    values = width * jax.random.normal(rng, extent, jnp.float32)
    if cuts:
        values = values * block_levels(rng, extent, cuts, -0.22, 0.18)
    return jnp.clip(values, -most, most).astype(held_as)


def setup_inputs(seed: int = 0) -> dict:
    splits = jax.random.split(jax.random.key(seed), 10)
    return {
        "layer_in": noise(splits[0], (TOKENS, D), 1.0, 6.0, ((0, 64), (1, 8))),
        "grad_out": noise(splits[1], (TOKENS, D), 1.0, 6.0, ((0, 64), (1, 8))),
        "gate_prob": jnp.clip(jnp.exp(math.log(0.6) - 2.4849067 * jax.random.uniform(splits[2], (TOKENS, TOP), jnp.float32) ** block_levels(splits[2], (TOKENS, TOP), ((0, 64),), -0.2, 0.2)), 0.05, 0.6),
        "expert_ids": draw_expert_ids(jax.random.fold_in(splits[9], 71), 0),
        "replica_index": draw_replica_index(jax.random.fold_in(splits[9], 71), 0),
        "slot_expert": draw_slot_expert(jax.random.fold_in(splits[9], 71), 0),
        "w_gate": draw_w_gate(jax.random.fold_in(splits[9], 71), 0),
        "w_up": draw_w_up(jax.random.fold_in(splits[9], 71), 0),
        "w_down": draw_w_down(jax.random.fold_in(splits[9], 71), 0),
    }


def reference(layer_in, grad_out, gate_prob, expert_ids, replica_index, slot_expert, w_gate, w_up, w_down):
    slot_index = jnp.arange(SLOTS, dtype=jnp.int32)
    expert_index = jnp.arange(EXPERTS, dtype=jnp.int32)
    is_start = slot_expert != jnp.roll(slot_expert, 1)
    first_slot = jnp.sum(jnp.where((slot_expert[None, :] == expert_index[:, None]) & is_start[None, :], slot_index[None, :], 0), axis=1).astype(jnp.int32)
    flat_slot = ((first_slot[expert_ids] + replica_index) % SLOTS).reshape(-1).astype(jnp.int32)
    flat_token = jnp.repeat(jnp.arange(TOKENS, dtype=jnp.int32), TOP)
    flat_prob = gate_prob.reshape(-1)
    ordering = jnp.argsort(flat_slot, stable=True).astype(jnp.int32)
    slot_counts = jnp.sum((flat_slot[None, :] == slot_index[:, None]).astype(jnp.int32), axis=1)
    slot_offsets = (jnp.cumsum(slot_counts) - slot_counts).astype(jnp.int32)
    group_size = FF // N_DP
    highest = lax.Precision.HIGHEST

    def one_slot(carry, slot_id):
        grad_total, expert_total = carry
        positions = slot_offsets[slot_id] + jnp.arange(RECV, dtype=jnp.int32)
        valid = jnp.arange(RECV, dtype=jnp.int32) < slot_counts[slot_id]
        picked = ordering[jnp.clip(positions, 0, TOKENS * TOP - 1)]
        token_rows = flat_token[picked]
        weight_rows = jnp.where(valid, flat_prob[picked], jnp.zeros((), flat_prob.dtype))
        inputs = jnp.where(valid[:, None], layer_in[token_rows], jnp.zeros((), layer_in.dtype))
        scaled = (weight_rows[:, None] * grad_out[token_rows].astype(jnp.float32)).astype(jnp.bfloat16)
        gate_matrix = w_gate[slot_id]
        up_matrix = w_up[slot_id]
        down_matrix = w_down[slot_id]
        gate_pre = jnp.dot(inputs, gate_matrix, preferred_element_type=jnp.float32)
        up_pre = jnp.dot(inputs, up_matrix, preferred_element_type=jnp.float32)
        hidden = (jax.nn.silu(gate_pre) * up_pre).astype(jnp.bfloat16)
        hidden_grad = lax.dot_general(scaled, down_matrix, (((1,), (1,)), ((), ())), preferred_element_type=jnp.float32)
        sigma = jax.nn.sigmoid(gate_pre)
        gate_grad = (hidden_grad * up_pre * sigma * (1.0 + gate_pre * (1.0 - sigma))).astype(jnp.bfloat16)
        up_grad = (hidden_grad * gate_pre * sigma).astype(jnp.bfloat16)
        gate_groups = gate_grad.astype(jnp.float32).reshape(RECV, N_DP, group_size)
        up_groups = up_grad.astype(jnp.float32).reshape(RECV, N_DP, group_size)
        gate_weights = gate_matrix.astype(jnp.float32).reshape(D, N_DP, group_size)
        up_weights = up_matrix.astype(jnp.float32).reshape(D, N_DP, group_size)
        partial_value = jnp.einsum("rgh,dgh->rgd", gate_groups, gate_weights, precision=highest)
        partial_value = partial_value + jnp.einsum("rgh,dgh->rgd", up_groups, up_weights, precision=highest)
        partial_value = lax.optimization_barrier(partial_value.astype(jnp.bfloat16))
        row_grad = jnp.sum(partial_value.astype(jnp.float32), axis=1)
        row_grad = jnp.where(valid[:, None], row_grad, jnp.zeros((), row_grad.dtype))
        grad_total = grad_total.at[token_rows].add(row_grad)
        slot_partial = lax.dot_general(hidden, scaled, (((0,), (0,)), ((), ())), preferred_element_type=jnp.float32)
        slot_partial = lax.optimization_barrier(slot_partial.astype(jnp.bfloat16))
        expert_total = expert_total.at[slot_expert[slot_id]].add(slot_partial.astype(jnp.float32))
        return (grad_total, expert_total), None

    start = (jnp.zeros((TOKENS, D), jnp.float32), jnp.zeros((EXPERTS, FF, D), jnp.float32))
    (grad_total, expert_total), unused = lax.scan(one_slot, start, slot_index)
    grad_in = grad_total.astype(jnp.bfloat16)
    grad_w_down = expert_total.astype(jnp.bfloat16)[slot_expert]
    return (grad_in, grad_w_down)
```

```python
import jax
import jax.numpy as jnp
from jax import lax
from jax.sharding import PartitionSpec as P

TOP = 8


def passed_along(value, axis, steps):
    count = lax.axis_size(axis)
    pairs = [(source, (source + steps) % count) for source in range(count)]
    return lax.ppermute(value, axis, pairs)


def body(
    layer_in, grad_out, gate_prob, expert_ids, replica_index, slot_expert, w_gate, w_up, w_down
):
    slots = lax.axis_size("expert")
    maxrep = min(4, slots // 8)
    tok_count = layer_in.shape[0]
    capacity = tok_count // maxrep
    recv_rows = slots * capacity
    expert_count = (8 - maxrep) * slots // 8
    slot_index = jnp.arange(slots, dtype=jnp.int32)
    expert_index = jnp.arange(expert_count, dtype=jnp.int32)
    is_start = slot_expert != jnp.roll(slot_expert, 1)
    first_slot = jnp.sum(
        jnp.where(
            (slot_expert[None, :] == expert_index[:, None]) & is_start[None, :],
            slot_index[None, :],
            0,
        ),
        axis=1,
    )
    expert_flat = expert_ids.reshape(-1)
    route_slot = jnp.sum(
        jnp.where(expert_flat[:, None] == expert_index[None, :], first_slot[None, :], 0), axis=1
    )
    route_slot = (route_slot + replica_index.reshape(-1)) % slots
    onehot = (route_slot[:, None] == slot_index[None, :]).astype(jnp.int32)
    rank_in_slot = jnp.sum((jnp.cumsum(onehot, axis=0) - onehot) * onehot, axis=1)
    position = route_slot * capacity + rank_in_slot
    prob_flat = gate_prob.reshape(-1)

    def pack(values):
        buffer = jnp.zeros((recv_rows, values.shape[1]), values.dtype).at[position].set(values)
        return buffer.reshape(slots, capacity, values.shape[1])

    repeated = jnp.repeat(grad_out, TOP, axis=0).astype(jnp.float32)
    inputs, scaled = (
        lax.all_gather(
            lax.all_to_all(
                pack(jnp.repeat(layer_in, TOP, axis=0)),
                "expert",
                split_axis=0,
                concat_axis=0,
                tiled=True,
            ),
            "dp",
            axis=2,
            tiled=True,
        ),
        lax.all_gather(
            lax.all_to_all(
                pack((prob_flat[:, None] * repeated).astype(jnp.bfloat16)),
                "expert",
                split_axis=0,
                concat_axis=0,
                tiled=True,
            ),
            "dp",
            axis=2,
            tiled=True,
        ),
    )
    inputs = inputs.reshape(recv_rows, -1)
    scaled = scaled.reshape(recv_rows, -1)
    width = inputs.shape[1]
    gate_matrix = w_gate[0]
    up_matrix = w_up[0]
    down_matrix = w_down[0]
    gate_pre = jnp.dot(inputs, gate_matrix, preferred_element_type=jnp.float32)
    up_pre = jnp.dot(inputs, up_matrix, preferred_element_type=jnp.float32)
    hidden = (jax.nn.silu(gate_pre) * up_pre).astype(jnp.bfloat16)
    contract_last = (((1,), (1,)), ((), ()))
    hidden_grad = lax.dot_general(
        scaled, down_matrix, contract_last, preferred_element_type=jnp.float32
    )
    sigma = jax.nn.sigmoid(gate_pre)
    gate_grad = (hidden_grad * up_pre * sigma * (1.0 + gate_pre * (1.0 - sigma))).astype(
        jnp.bfloat16
    )
    up_grad = (hidden_grad * gate_pre * sigma).astype(jnp.bfloat16)
    partial_value = lax.dot_general(
        gate_grad, gate_matrix, contract_last, preferred_element_type=jnp.float32
    )
    partial_value = partial_value + lax.dot_general(
        up_grad, up_matrix, contract_last, preferred_element_type=jnp.float32
    )
    partial_value = partial_value.reshape(slots, capacity, width)
    summed = lax.psum_scatter(
        partial_value.astype(jnp.bfloat16), "dp", scatter_dimension=2, tiled=True
    ).astype(jnp.float32)
    returned = lax.all_to_all(
        summed.astype(jnp.bfloat16), "expert", split_axis=0, concat_axis=0, tiled=True
    ).astype(summed.dtype)
    flat_back = returned.reshape(recv_rows, -1)
    grad_in = jnp.sum(flat_back[position].reshape(tok_count, TOP, -1), axis=1).astype(jnp.bfloat16)
    slot_partial = lax.dot_general(
        hidden, scaled, (((0,), (0,)), ((), ())), preferred_element_type=jnp.float32
    ).astype(jnp.bfloat16)
    own_index = lax.axis_index("expert")
    expert_here = jnp.sum(jnp.where(slot_index == own_index, slot_expert, 0))

    def same_at(offset):
        neighbour = (own_index - offset) % slots
        match = jnp.any((slot_index == neighbour) & (slot_expert == expert_here))
        return match.astype(jnp.float32)

    own = slot_partial.astype(jnp.float32)
    left = own + same_at(1) * passed_along(slot_partial, "expert", 1).astype(jnp.float32)
    right = own + same_at(-1) * passed_along(slot_partial, "expert", -1).astype(jnp.float32)
    far_left = passed_along(left.astype(jnp.bfloat16), "expert", 2).astype(jnp.float32)
    far_right = passed_along(right.astype(jnp.bfloat16), "expert", -2).astype(jnp.float32)
    total = left + same_at(2) * far_left + (right - own) + same_at(-2) * far_right
    grad_w_down = total.astype(jnp.bfloat16)[None]
    return (grad_in, grad_w_down)


def solution(mesh):
    placed = (
        P("expert", "dp"),
        P("expert", "dp"),
        P("expert", None),
        P("expert", None),
        P("expert", None),
        P(),
        P("expert", None, "dp"),
        P("expert", None, "dp"),
        P("expert", "dp", None),
    )
    return jax.shard_map(
        body,
        mesh=mesh,
        in_specs=placed,
        out_specs=(P("expert", "dp"), P("expert", "dp", None)),
        check_vma=False,
    )
```

```python
import jax
import jax.numpy as jnp
from jax import lax
from jax.sharding import PartitionSpec as P

TOP = 8


def passed_along(value, axis, steps):
    count = lax.axis_size(axis)
    pairs = [(source, (source + steps) % count) for source in range(count)]
    return lax.ppermute(value, axis, pairs)


def body(
    layer_in, grad_out, gate_prob, expert_ids, replica_index, slot_expert, w_gate, w_up, w_down
):
    slots = lax.axis_size("expert")
    maxrep = min(4, slots // 8)
    tok_count = layer_in.shape[0]
    capacity = tok_count // maxrep
    recv_rows = slots * capacity
    expert_count = (8 - maxrep) * slots // 8
    slot_index = jnp.arange(slots, dtype=jnp.int32)
    expert_index = jnp.arange(expert_count, dtype=jnp.int32)
    is_start = slot_expert != jnp.roll(slot_expert, 1)
    first_slot = jnp.sum(
        jnp.where(
            (slot_expert[None, :] == expert_index[:, None]) & is_start[None, :],
            slot_index[None, :],
            0,
        ),
        axis=1,
    )
    own_index = lax.axis_index("expert")

    def route(ids, replicas):
        first = jnp.sum(
            jnp.where(ids[..., None] == expert_index, first_slot, 0), axis=-1
        )
        return (first + replicas) % slots

    codes = (expert_ids * 8 + replica_index).astype(jnp.float32)
    words = jnp.concatenate([codes, gate_prob], axis=1)
    all_words = lax.all_gather(words, "expert", axis=0, tiled=True)
    all_codes = all_words[:, :TOP].astype(jnp.int32)
    all_prob = all_words[:, TOP:]
    all_inputs = lax.all_gather(layer_in, "expert", axis=0, tiled=True)
    all_grads = lax.all_gather(grad_out, "expert", axis=0, tiled=True)

    here = route(all_codes // 8, all_codes % 8) == own_index
    prob_here = jnp.sum(jnp.where(here, all_prob, 0.0), axis=1)
    chosen = jnp.any(here, axis=1).astype(jnp.int32).reshape(slots, tok_count)
    rank = jnp.cumsum(chosen, axis=1) - chosen
    row = jnp.where(chosen > 0, slot_index[:, None] * capacity + rank, -1).reshape(-1)
    pick = (jnp.arange(recv_rows, dtype=jnp.int32)[:, None] == row[None, :]).astype(jnp.bfloat16)

    def picked(values):
        rows = jnp.dot(pick, values, preferred_element_type=jnp.float32).astype(jnp.bfloat16)
        return lax.all_gather(rows, "dp", axis=1, tiled=True)

    inputs = picked(all_inputs)
    scaled = picked((prob_here[:, None] * all_grads.astype(jnp.float32)).astype(jnp.bfloat16))
    width = inputs.shape[1]
    gate_matrix = w_gate[0]
    up_matrix = w_up[0]
    down_matrix = w_down[0]
    gate_pre = jnp.dot(inputs, gate_matrix, preferred_element_type=jnp.float32)
    up_pre = jnp.dot(inputs, up_matrix, preferred_element_type=jnp.float32)
    hidden = (jax.nn.silu(gate_pre) * up_pre).astype(jnp.bfloat16)
    contract_last = (((1,), (1,)), ((), ()))
    hidden_grad = lax.dot_general(
        scaled, down_matrix, contract_last, preferred_element_type=jnp.float32
    )
    sigma = jax.nn.sigmoid(gate_pre)
    gate_grad = (hidden_grad * up_pre * sigma * (1.0 + gate_pre * (1.0 - sigma))).astype(
        jnp.bfloat16
    )
    up_grad = (hidden_grad * gate_pre * sigma).astype(jnp.bfloat16)
    partial_value = lax.dot_general(
        gate_grad, gate_matrix, contract_last, preferred_element_type=jnp.float32
    )
    partial_value = partial_value + lax.dot_general(
        up_grad, up_matrix, contract_last, preferred_element_type=jnp.float32
    )
    partial_value = partial_value.reshape(slots, capacity, width)
    summed = lax.psum_scatter(
        partial_value.astype(jnp.bfloat16), "dp", scatter_dimension=2, tiled=True
    )
    returned = lax.all_to_all(
        summed, "expert", split_axis=0, concat_axis=0, tiled=True
    )
    flat_back = returned.reshape(recv_rows, -1)
    route_slot = route(expert_ids, replica_index)
    onehot = jnp.any(route_slot[:, :, None] == slot_index, axis=1).astype(jnp.int32)
    rank_back = jnp.cumsum(onehot, axis=0) - onehot
    place = jnp.arange(capacity, dtype=jnp.int32)
    unpick = ((onehot[:, :, None] > 0) & (rank_back[:, :, None] == place)).astype(jnp.bfloat16)
    grad_in = jnp.dot(
        unpick.reshape(tok_count, recv_rows), flat_back, preferred_element_type=jnp.float32
    ).astype(jnp.bfloat16)
    slot_partial = lax.dot_general(
        hidden, scaled, (((0,), (0,)), ((), ())), preferred_element_type=jnp.float32
    ).astype(jnp.bfloat16)
    expert_here = jnp.sum(jnp.where(slot_index == own_index, slot_expert, 0))

    def same_at(offset):
        neighbour = (own_index - offset) % slots
        match = jnp.any((slot_index == neighbour) & (slot_expert == expert_here))
        return match.astype(jnp.float32)

    own = slot_partial.astype(jnp.float32)
    left = own + same_at(1) * passed_along(slot_partial, "expert", 1).astype(jnp.float32)
    right = own + same_at(-1) * passed_along(slot_partial, "expert", -1).astype(jnp.float32)
    far_left = passed_along(left.astype(jnp.bfloat16), "expert", 2).astype(jnp.float32)
    far_right = passed_along(right.astype(jnp.bfloat16), "expert", -2).astype(jnp.float32)
    total = left + same_at(2) * far_left + (right - own) + same_at(-2) * far_right
    grad_w_down = total.astype(jnp.bfloat16)[None]
    return (grad_in, grad_w_down)


def solution(mesh):
    placed = (
        P("expert", "dp"),
        P("expert", "dp"),
        P("expert", None),
        P("expert", None),
        P("expert", None),
        P(),
        P("expert", None, "dp"),
        P("expert", None, "dp"),
        P("expert", "dp", None),
    )
    return jax.shard_map(
        body,
        mesh=mesh,
        in_specs=placed,
        out_specs=(P("expert", "dp"), P("expert", "dp", None)),
        check_vma=False,
    )
```

```python
import jax
import jax.numpy as jnp
from jax import lax
from jax.sharding import PartitionSpec as P

TOP = 8


def passed_along(value, axis, steps):
    count = lax.axis_size(axis)
    pairs = [(source, (source + steps) % count) for source in range(count)]
    return lax.ppermute(value, axis, pairs)


def body(
    layer_in, grad_out, gate_prob, expert_ids, replica_index, slot_expert, w_gate, w_up, w_down
):
    slots = lax.axis_size("expert")
    maxrep = min(4, slots // 8)
    tok_count = layer_in.shape[0]
    capacity = tok_count // maxrep
    recv_rows = slots * capacity
    expert_count = (8 - maxrep) * slots // 8
    slot_index = jnp.arange(slots, dtype=jnp.int32)
    expert_index = jnp.arange(expert_count, dtype=jnp.int32)
    is_start = slot_expert != jnp.roll(slot_expert, 1)
    first_slot = jnp.sum(
        jnp.where(
            (slot_expert[None, :] == expert_index[:, None]) & is_start[None, :],
            slot_index[None, :],
            0,
        ),
        axis=1,
    )
    expert_flat = expert_ids.reshape(-1)
    route_slot = jnp.sum(
        jnp.where(expert_flat[:, None] == expert_index[None, :], first_slot[None, :], 0), axis=1
    )
    route_slot = (route_slot + replica_index.reshape(-1)) % slots
    onehot = (route_slot[:, None] == slot_index[None, :]).astype(jnp.int32)
    rank_in_slot = jnp.sum((jnp.cumsum(onehot, axis=0) - onehot) * onehot, axis=1)
    position = route_slot * capacity + rank_in_slot
    prob_flat = gate_prob.reshape(-1)

    def pack(values):
        buffer = jnp.zeros((recv_rows, values.shape[1]), values.dtype).at[position].set(values)
        return buffer.reshape(slots, capacity, values.shape[1])

    repeated = jnp.repeat(grad_out, TOP, axis=0).astype(jnp.float32)
    inputs, scaled = (
        lax.all_gather(
            lax.all_to_all(
                pack(jnp.repeat(layer_in, TOP, axis=0)),
                "expert",
                split_axis=0,
                concat_axis=0,
                tiled=True,
            ),
            "dp",
            axis=2,
            tiled=True,
        ),
        lax.all_gather(
            lax.all_to_all(
                pack((prob_flat[:, None] * repeated).astype(jnp.bfloat16)),
                "expert",
                split_axis=0,
                concat_axis=0,
                tiled=True,
            ),
            "dp",
            axis=2,
            tiled=True,
        ),
    )
    inputs = inputs.reshape(recv_rows, -1)
    scaled = scaled.reshape(recv_rows, -1)
    width = inputs.shape[1]
    gate_matrix = w_gate[0]
    up_matrix = w_up[0]
    down_matrix = w_down[0]
    gate_pre = jnp.dot(inputs, gate_matrix, preferred_element_type=jnp.float32)
    up_pre = jnp.dot(inputs, up_matrix, preferred_element_type=jnp.float32)
    hidden = (jax.nn.silu(gate_pre) * up_pre).astype(jnp.bfloat16)
    slot_partial = lax.dot_general(
        hidden, scaled, (((0,), (0,)), ((), ())), preferred_element_type=jnp.float32
    ).astype(jnp.bfloat16)
    slot_partial, scaled = lax.optimization_barrier((slot_partial, scaled))
    contract_last = (((1,), (1,)), ((), ()))
    hidden_grad = lax.dot_general(
        scaled, down_matrix, contract_last, preferred_element_type=jnp.float32
    )
    sigma = jax.nn.sigmoid(gate_pre)
    gate_grad = (hidden_grad * up_pre * sigma * (1.0 + gate_pre * (1.0 - sigma))).astype(
        jnp.bfloat16
    )
    up_grad = (hidden_grad * gate_pre * sigma).astype(jnp.bfloat16)
    partial_value = lax.dot_general(
        gate_grad, gate_matrix, contract_last, preferred_element_type=jnp.float32
    )
    partial_value = partial_value + lax.dot_general(
        up_grad, up_matrix, contract_last, preferred_element_type=jnp.float32
    )
    partial_value = partial_value.reshape(slots, capacity, width)
    summed = lax.psum_scatter(
        partial_value.astype(jnp.bfloat16), "dp", scatter_dimension=2, tiled=True
    ).astype(jnp.float32)
    returned = lax.all_to_all(
        summed.astype(jnp.bfloat16), "expert", split_axis=0, concat_axis=0, tiled=True
    ).astype(summed.dtype)
    flat_back = returned.reshape(recv_rows, -1)
    grad_in = jnp.sum(flat_back[position].reshape(tok_count, TOP, -1), axis=1).astype(jnp.bfloat16)
    own_index = lax.axis_index("expert")
    expert_here = jnp.sum(jnp.where(slot_index == own_index, slot_expert, 0))

    def same_at(offset):
        neighbour = (own_index - offset) % slots
        match = jnp.any((slot_index == neighbour) & (slot_expert == expert_here))
        return match.astype(jnp.float32)

    own = slot_partial.astype(jnp.float32)
    left = own + same_at(1) * passed_along(slot_partial, "expert", 1).astype(jnp.float32)
    right = own + same_at(-1) * passed_along(slot_partial, "expert", -1).astype(jnp.float32)
    far_left = passed_along(left.astype(jnp.bfloat16), "expert", 2).astype(jnp.float32)
    far_right = passed_along(right.astype(jnp.bfloat16), "expert", -2).astype(jnp.float32)
    total = left + same_at(2) * far_left + (right - own) + same_at(-2) * far_right
    grad_w_down = total.astype(jnp.bfloat16)[None]
    return (grad_in, grad_w_down)


def solution(mesh):
    placed = (
        P("expert", "dp"),
        P("expert", "dp"),
        P("expert", None),
        P("expert", None),
        P("expert", None),
        P(),
        P("expert", None, "dp"),
        P("expert", None, "dp"),
        P("expert", "dp", None),
    )
    return jax.shard_map(
        body,
        mesh=mesh,
        in_specs=placed,
        out_specs=(P("expert", "dp"), P("expert", "dp", None)),
        check_vma=False,
    )
```
